32 devices in a mesh: space: 16 (over z, x, core), tm: 2 (over y).
Axes of the slice: x: 2, y: 2, z: 4, core: 2. Of those that a mesh axis runs over, the one named last changes fastest.
Arguments:
- thermal_anomaly: bfloat16 [128, 140288], P('tm', 'space'), may hold values from -6 to 6
- smoothing_coefs: float32 [128], replicated, may hold values from -0.0075 to 0.0075
Outputs:
- orthonormal_basis: float32 [128, 140288], P(None, ('space', 'tm'))
- triangular_factor: float32 [128, 128], replicated
The draws below stay inside these ranges and needn't reach their ends.
All inputs are finite; a program needn't handle non-finite values.
Results may differ from the reference program's by a relative error of at most 0.0003.
The reference program's roundings to bfloat16 on the way count: a program that leaves them out, or rounds other values in their place, can miss the bound.
Values may be sent and summed in bfloat16 or wider, within the bound.
A program may use at most 64 MiB of HBM per device.

```python
import math
import jax
import jax.numpy as jnp
from jax import lax

TAPS = 129
SPAN_TIMESTEPS = 128
SPATIAL_SITES = 140288


def draw_thermal_anomaly(key, part):
    keys = jax.random.split(jax.random.fold_in(key, 17), 5)
    count = 6
    hours = jnp.arange(SPAN_TIMESTEPS, dtype=jnp.float32)[:, None]
    cycles = jax.random.uniform(keys[0], (count,), jnp.float32, 0.5, 8.0)
    phases = jax.random.uniform(keys[1], (count,), jnp.float32, -math.pi, math.pi)
    root_three = math.sqrt(3.0)
    patterns = jax.random.uniform(keys[3], (count, SPATIAL_SITES), jnp.float32, -root_three, root_three)
    strengths = jnp.exp(jax.random.uniform(keys[2], (count,), jnp.float32, math.log(0.12), math.log(0.35)))
    noise = jax.random.truncated_normal(keys[4], -3.0, 3.0, (SPAN_TIMESTEPS, SPATIAL_SITES), jnp.float32)
    total = noise
    for index in range(count):
        temporal = math.sqrt(2.0) * jnp.cos(2.0 * math.pi * cycles[index] * hours / SPAN_TIMESTEPS + phases[index])
        total = total + strengths[index] * temporal * patterns[index][None, :]
    return jnp.clip(total, -6.0, 6.0).astype(jnp.bfloat16)


def setup_inputs(seed: int = 0) -> dict:
    key_list = jax.random.split(jax.random.key(seed), 3)
    thermal_anomaly = draw_thermal_anomaly(jax.random.fold_in(key_list[2], 71), 0)
    smoothing_coefs = jnp.clip(jax.random.uniform(key_list[1], (TAPS - 1,), jnp.float32, -0.0075, 0.0075), -0.0075, 0.0075)
    return dict(thermal_anomaly=thermal_anomaly, smoothing_coefs=smoothing_coefs)


def banded_matrix(coefficients, count_rows, count_cols, delay_shift_amount):
    row_index = lax.broadcasted_iota(jnp.int32, (count_rows, count_cols), 0)
    col_index = lax.broadcasted_iota(jnp.int32, (count_rows, count_cols), 1)
    lag_index = row_index + delay_shift_amount - col_index
    length = coefficients.shape[0]
    inside = (lag_index >= 0) & (lag_index < length)
    safe = jnp.clip(lag_index, 0, length - 1).astype(jnp.int32)
    return jnp.where(inside, coefficients[safe], jnp.zeros((), coefficients.dtype))

def reference(thermal_anomaly, smoothing_coefs):
    coefficients = jnp.concatenate([jnp.ones((1,), jnp.float32), smoothing_coefs.astype(jnp.float32)]).astype(jnp.bfloat16)
    snapshot_array = banded_matrix(coefficients, SPAN_TIMESTEPS, SPAN_TIMESTEPS, 0)
    averaged_record = jnp.dot(snapshot_array.astype(jnp.float32), thermal_anomaly.astype(jnp.float32), preferred_element_type=jnp.float32).astype(jnp.bfloat16)
    gram = jnp.dot(averaged_record.astype(jnp.float32), averaged_record.T.astype(jnp.float32), preferred_element_type=jnp.float32)
    lower_one = jnp.linalg.cholesky(gram)
    first_rows = jax.scipy.linalg.solve_triangular(lower_one, averaged_record.astype(jnp.float32), lower=True)
    scale = jnp.sqrt(jnp.float32(SPATIAL_SITES))
    return (first_rows * scale, lower_one / scale)
```

```python
import functools
import math

import jax
import jax.numpy as jnp
from jax import lax
from jax.experimental import pallas as pl
from jax.experimental.pallas import tpu as pltpu
from jax.sharding import PartitionSpec as P

LANES = 128
SUB = 8
PLANE = 4
CHUNKS = 5
MESH = pl.DeviceIdType.MESH


def banded(coefficients, rows, cols, delay):
    lag = (
        lax.broadcasted_iota(jnp.int32, (rows, cols), 0)
        + delay
        - lax.broadcasted_iota(jnp.int32, (rows, cols), 1)
    )
    one_hot = lag[:, :, None] == lax.broadcasted_iota(
        jnp.int32, (1, 1, coefficients.shape[0]), 2
    )
    return jnp.sum(jnp.where(one_hot, coefficients.astype(jnp.float32), 0.0), axis=2).astype(
        coefficients.dtype
    )


def general_body(thermal_anomaly, smoothing_coefs):
    steps = thermal_anomaly.shape[0]
    blocks = lax.axis_size("tm")
    coefficients = jnp.concatenate([jnp.ones((1,), jnp.float32), smoothing_coefs]).astype(
        jnp.bfloat16
    )
    reach = min(blocks - 1, -(-(coefficients.shape[0] - 1) // steps))
    record = [thermal_anomaly]
    for distance in range(1, reach + 1):
        route = [(i, i + distance) for i in range(blocks - distance)]
        record.insert(0, lax.ppermute(thermal_anomaly, "tm", route))
    matrix = banded(coefficients, steps, (reach + 1) * steps, reach * steps)
    outgoing = jnp.dot(
        matrix, jnp.concatenate(record, axis=0), preferred_element_type=jnp.float32
    ).astype(jnp.bfloat16)
    arrived = lax.all_to_all(outgoing, "tm", split_axis=1, concat_axis=0, tiled=True)
    gram = lax.psum(
        jnp.dot(arrived, arrived.T, preferred_element_type=jnp.float32), ("space", "tm")
    )
    lower = jnp.linalg.cholesky(gram)
    rows = jax.scipy.linalg.solve_triangular(lower, arrived.astype(jnp.float32), lower=True)
    scale = jnp.sqrt(jnp.float32(thermal_anomaly.shape[1] * lax.axis_size("space")))
    return rows * scale, lower / scale


def place(dst, rows, x_ref, base, start, width, half):
    valid = min(width, half - start)
    low = base + start
    aligned = low // LANES * LANES
    shift = low - aligned
    end = min(aligned + pl.cdiv(shift + valid, LANES) * LANES, x_ref.shape[1])
    value = x_ref[:, aligned:end][:, shift : shift + valid]
    if valid < width:
        edge = valid // LANES * LANES
        dst[rows, start + edge : start + width] = jnp.zeros(
            (value.shape[0], width - edge), dst.dtype
        )
    dst[rows, start : start + valid] = value


def gather_kernel(
    spans,
    x_ref,
    coef_ref,
    filtered_ref,
    gram_ref,
    outgoing,
    panel,
    partial,
    pieces,
    reduced,
    planes,
    whole,
    swap_send,
    swap_recv,
    rs_send,
    rs_recv,
    line_send,
    line_recv,
    ag_send,
    ag_recv,
):
    space = lax.axis_index("space")
    tm = lax.axis_index("tm")
    inner = space % PLANE
    plane = space // PLANE
    lines = lax.axis_size("space") // PLANE
    group = PLANE * 2
    me = inner * 2 + tm
    hours = x_ref.shape[0]
    total = 2 * hours
    half = x_ref.shape[1] // 2
    share = total // group

    def in_group(offset):
        other = (me + offset) % group
        return other, (plane * PLANE + other // 2, other % 2)

    def in_line(offset):
        return ((plane + offset) % lines * PLANE + inner, tm)

    barrier = pltpu.get_barrier_semaphore()
    for offset in range(1, group):
        pl.semaphore_signal(barrier, inc=1, device_id=in_group(offset)[1], device_id_type=MESH)
    for offset in range(1, lines):
        pl.semaphore_signal(barrier, inc=1, device_id=in_line(offset), device_id_type=MESH)

    for side in range(2):

        @pl.when(tm == side)
        def _():
            for start, width in spans:
                place(outgoing, slice(None), x_ref, (1 - side) * half, start, width, half)

    pl.semaphore_wait(barrier, group - 1 + lines - 1)

    swaps = []
    for index, (start, width) in enumerate(spans):
        copy = pltpu.make_async_remote_copy(
            src_ref=outgoing.at[:, pl.ds(start, width)],
            dst_ref=panel.at[pl.ds(pl.multiple_of(tm * hours, hours), hours), pl.ds(start, width)],
            send_sem=swap_send.at[index],
            recv_sem=swap_recv.at[index],
            device_id=(space, 1 - tm),
            device_id_type=MESH,
        )
        copy.start()
        swaps.append(copy)

    for side in range(2):

        @pl.when(tm == side)
        def _():
            rows = slice(side * hours, (side + 1) * hours)
            for start, width in spans:
                place(panel, rows, x_ref, side * half, start, width, half)

    row = lax.broadcasted_iota(jnp.int32, (total, total), 0)
    col = lax.broadcasted_iota(jnp.int32, (total, total), 1)
    lagged = jnp.broadcast_to(coef_ref[...], (total, total))
    lagged = pltpu.roll(lagged, 1, axis=1, stride=1, stride_axis=0)
    turned = jnp.where(col > row, lagged, jnp.where(col == row, 1.0, 0.0))
    matrix = turned.T.astype(jnp.bfloat16)

    partial[...] = jnp.zeros_like(partial)
    for index, (start, width) in enumerate(spans):
        swaps[index].wait_recv()
        values = jnp.dot(
            matrix, panel[:, start : start + width], preferred_element_type=jnp.float32
        ).astype(jnp.bfloat16)
        filtered_ref[:, start : start + width] = values
        partial[...] += lax.dot_general(
            values, values, (((1,), (1,)), ((), ())), preferred_element_type=jnp.float32
        )

    copies = []
    for offset in range(1, group):
        other, device = in_group(offset)
        copy = pltpu.make_async_remote_copy(
            src_ref=partial.at[pl.ds(pl.multiple_of(other * share, share), share)],
            dst_ref=pieces.at[offset - 1],
            send_sem=rs_send.at[offset - 1],
            recv_sem=rs_recv.at[offset - 1],
            device_id=device,
            device_id_type=MESH,
        )
        copy.start()
        copies.append(copy)
    mine = pl.ds(pl.multiple_of(me * share, share), share)
    running = partial[mine, :]
    for offset in range(1, group):
        copies[offset - 1].wait_recv()
        running = running + pieces[offset - 1]
    reduced[...] = running
    planes[plane] = running

    for offset in range(1, lines):
        copy = pltpu.make_async_remote_copy(
            src_ref=reduced,
            dst_ref=planes.at[plane],
            send_sem=line_send.at[offset - 1],
            recv_sem=line_recv.at[offset - 1],
            device_id=in_line(offset),
            device_id_type=MESH,
        )
        copy.start()
        copies.append(copy)
    for offset in range(1, lines):
        copies[group - 1 + offset - 1].wait_recv()
    running = planes[0]
    for index in range(1, lines):
        running = running + planes[index]
    whole[mine, :] = running

    for offset in range(1, group):
        copy = pltpu.make_async_remote_copy(
            src_ref=whole.at[mine],
            dst_ref=whole.at[mine],
            send_sem=ag_send.at[offset - 1],
            recv_sem=ag_recv.at[offset - 1],
            device_id=in_group(offset)[1],
            device_id_type=MESH,
        )
        copy.start()
        copies.append(copy)
    for copy in copies[-(group - 1) :]:
        copy.wait_recv()
    gram_ref[...] = whole[...]
    for copy in swaps + copies:
        copy.wait_send()


def factor(gram_ref, points):
    size = gram_ref.shape[0]
    count = size // SUB
    blocks = [gram_ref[SUB * b : SUB * (b + 1), :] for b in range(count)]
    lane = lax.broadcasted_iota(jnp.int32, (SUB, size), 1)
    sub = lax.broadcasted_iota(jnp.int32, (SUB, size), 0)
    pivots = [jnp.zeros((SUB, size), jnp.float32) for _ in range(count)]
    for k in range(size):
        b, r = divmod(k, SUB)
        columns = [
            jnp.broadcast_to(blocks[i][:, k : k + 1], (SUB, size)) for i in range(b, count)
        ]
        pivot = jnp.broadcast_to(columns[0][r : r + 1, :], (SUB, size))
        row = jnp.broadcast_to(blocks[b][r : r + 1, :], (SUB, size))
        pivots[b] = jnp.where(sub == r, pivot, pivots[b])
        here = lane == k
        ratio = jnp.where(here, 1.0, row) / pivot
        for i in range(b, count):
            new = jnp.where(here, 0.0, blocks[i]) - columns[i - b] * ratio
            blocks[i] = jnp.where(sub > r, new, blocks[i]) if i == b else new
    return blocks, pivots


def basis_kernel(points, gram_ref, filtered_ref, basis_ref, factor_ref, high, low, upper):
    @pl.when(pl.program_id(0) == 0)
    def _():
        size = gram_ref.shape[0]
        blocks, pivots = factor(gram_ref, points)
        lane = lax.broadcasted_iota(jnp.int32, (SUB, size), 1)
        sub = lax.broadcasted_iota(jnp.int32, (SUB, size), 0)
        root = math.sqrt(points)
        for b, (block, pivot) in enumerate(zip(blocks, pivots)):
            diagonal = jnp.sqrt(pivot)
            here = lane == sub + b * SUB
            below = lane < sub + b * SUB
            inverse = jnp.where(here, 1.0, jnp.where(below, block, 0.0)) * (root / diagonal)
            rows = slice(b * SUB, (b + 1) * SUB)
            top = inverse.astype(jnp.bfloat16).astype(jnp.float32)
            high[rows, :] = top
            low[rows, :] = inverse - top
            upper[rows, :] = jnp.where(here, pivot, jnp.where(below, 0.0, block)) / (
                diagonal * root
            )
        factor_ref[...] = upper[...].T

    values = filtered_ref[...]
    basis_ref[...] = jnp.dot(
        high[...].astype(jnp.bfloat16), values, preferred_element_type=jnp.float32
    ) + jnp.dot(low[...].astype(jnp.bfloat16), values, preferred_element_type=jnp.float32)


def paired_body(thermal_anomaly, smoothing_coefs):
    hours, sites = thermal_anomaly.shape
    total = 2 * hours
    half = sites // 2
    tiles = pl.cdiv(half, LANES)
    step = pl.cdiv(tiles, CHUNKS)
    spans = [
        (t * LANES, min(step, tiles - t) * LANES) for t in range(0, tiles, step)
    ]
    padded = tiles * LANES
    group = PLANE * 2
    lines = lax.axis_size("space") // PLANE
    share = total // group
    dma = pltpu.SemaphoreType.DMA
    vmem = pl.BlockSpec(memory_space=pltpu.VMEM)
    filtered, gram = pl.pallas_call(
        functools.partial(gather_kernel, spans),
        out_shape=(
            jax.ShapeDtypeStruct((total, padded), jnp.bfloat16),
            jax.ShapeDtypeStruct((total, total), jnp.float32),
        ),
        in_specs=[vmem, vmem],
        out_specs=(vmem, vmem),
        scratch_shapes=[
            pltpu.VMEM((hours, padded), jnp.bfloat16),
            pltpu.VMEM((total, padded), jnp.bfloat16),
            pltpu.VMEM((total, total), jnp.float32),
            pltpu.VMEM((group - 1, share, total), jnp.float32),
            pltpu.VMEM((share, total), jnp.float32),
            pltpu.VMEM((lines, share, total), jnp.float32),
            pltpu.VMEM((total, total), jnp.float32),
            dma((len(spans),)),
            dma((len(spans),)),
            dma((group - 1,)),
            dma((group - 1,)),
            dma((lines - 1,)),
            dma((lines - 1,)),
            dma((group - 1,)),
            dma((group - 1,)),
        ],
        compiler_params=pltpu.CompilerParams(collective_id=0, has_side_effects=True),
        name="gather_gram",
    )(thermal_anomaly, smoothing_coefs[: total].reshape(1, total))

    width = step * LANES
    points = sites * lax.axis_size("space")
    return pl.pallas_call(
        functools.partial(basis_kernel, points),
        grid=(pl.cdiv(half, width),),
        out_shape=(
            jax.ShapeDtypeStruct((total, half), jnp.float32),
            jax.ShapeDtypeStruct((total, total), jnp.float32),
        ),
        in_specs=[
            pl.BlockSpec((total, total), lambda i: (0, 0)),
            pl.BlockSpec((total, width), lambda i: (0, i)),
        ],
        out_specs=(
            pl.BlockSpec((total, width), lambda i: (0, i)),
            pl.BlockSpec((total, total), lambda i: (0, 0)),
        ),
        scratch_shapes=[pltpu.VMEM((total, total), jnp.float32)] * 3,
        name="factor_basis",
    )(gram, filtered)


def body(thermal_anomaly, smoothing_coefs):
    hours, sites = thermal_anomaly.shape
    paired = (
        lax.axis_size("tm") == 2
        and 2 * hours == LANES
        and smoothing_coefs.shape[0] >= LANES
        and sites % 2 == 0
        and lax.axis_size("space") % PLANE == 0
        and lax.axis_size("space") > PLANE
    )
    return (paired_body if paired else general_body)(thermal_anomaly, smoothing_coefs)


def solution(mesh):
    placed = (P("tm", "space"), P())
    return jax.shard_map(
        body, mesh=mesh, in_specs=placed, out_specs=(P(None, ("space", "tm")), P()), check_vma=False
    )
```

```python
import functools
import math

import jax
import jax.numpy as jnp
from jax import lax
from jax.experimental import pallas as pl
from jax.experimental.pallas import tpu as pltpu
from jax.sharding import PartitionSpec as P

LANES = 128
SUB = 8
PLANE = 4
CHUNKS = 5
MESH = pl.DeviceIdType.MESH


def banded(coefficients, rows, cols, delay):
    lag = (
        lax.broadcasted_iota(jnp.int32, (rows, cols), 0)
        + delay
        - lax.broadcasted_iota(jnp.int32, (rows, cols), 1)
    )
    one_hot = lag[:, :, None] == lax.broadcasted_iota(
        jnp.int32, (1, 1, coefficients.shape[0]), 2
    )
    return jnp.sum(jnp.where(one_hot, coefficients.astype(jnp.float32), 0.0), axis=2).astype(
        coefficients.dtype
    )


def general_body(thermal_anomaly, smoothing_coefs):
    steps = thermal_anomaly.shape[0]
    blocks = lax.axis_size("tm")
    coefficients = jnp.concatenate([jnp.ones((1,), jnp.float32), smoothing_coefs]).astype(
        jnp.bfloat16
    )
    reach = min(blocks - 1, -(-(coefficients.shape[0] - 1) // steps))
    record = [thermal_anomaly]
    for distance in range(1, reach + 1):
        route = [(i, i + distance) for i in range(blocks - distance)]
        record.insert(0, lax.ppermute(thermal_anomaly, "tm", route))
    matrix = banded(coefficients, steps, (reach + 1) * steps, reach * steps)
    outgoing = jnp.dot(
        matrix, jnp.concatenate(record, axis=0), preferred_element_type=jnp.float32
    ).astype(jnp.bfloat16)
    arrived = lax.all_to_all(outgoing, "tm", split_axis=1, concat_axis=0, tiled=True)
    gram = lax.psum(
        jnp.dot(arrived, arrived.T, preferred_element_type=jnp.float32), ("space", "tm")
    )
    lower = jnp.linalg.cholesky(gram)
    rows = jax.scipy.linalg.solve_triangular(lower, arrived.astype(jnp.float32), lower=True)
    scale = jnp.sqrt(jnp.float32(thermal_anomaly.shape[1] * lax.axis_size("space")))
    return rows * scale, lower / scale


def place(dst, rows, x_ref, base, start, width, half):
    valid = min(width, half - start)
    low = base + start
    aligned = low // LANES * LANES
    shift = low - aligned
    end = min(aligned + pl.cdiv(shift + valid, LANES) * LANES, x_ref.shape[1])
    value = x_ref[:, aligned:end][:, shift : shift + valid]
    if valid < width:
        edge = valid // LANES * LANES
        dst[rows, start + edge : start + width] = jnp.zeros(
            (value.shape[0], width - edge), dst.dtype
        )
    dst[rows, start : start + valid] = value


def gather_kernel(
    spans,
    x_ref,
    coef_ref,
    filtered_ref,
    gram_ref,
    outgoing,
    panel,
    partial,
    pieces,
    reduced,
    planes,
    whole,
    swap_send,
    swap_recv,
    rs_send,
    rs_recv,
    line_send,
    line_recv,
    ag_send,
    ag_recv,
):
    space = lax.axis_index("space")
    tm = lax.axis_index("tm")
    inner = space % PLANE
    plane = space // PLANE
    lines = lax.axis_size("space") // PLANE
    group = PLANE * 2
    me = inner * 2 + tm
    hours = x_ref.shape[0]
    total = 2 * hours
    half = x_ref.shape[1] // 2
    share = total // group

    def in_group(offset):
        other = (me + offset) % group
        return other, (plane * PLANE + other // 2, other % 2)

    def in_line(offset):
        return ((plane + offset) % lines * PLANE + inner, tm)

    barrier = pltpu.get_barrier_semaphore()
    for offset in range(1, group):
        pl.semaphore_signal(barrier, inc=1, device_id=in_group(offset)[1], device_id_type=MESH)
    for offset in range(1, lines):
        pl.semaphore_signal(barrier, inc=1, device_id=in_line(offset), device_id_type=MESH)

    for side in range(2):

        @pl.when(tm == side)
        def _():
            for start, width in spans:
                place(outgoing, slice(None), x_ref, (1 - side) * half, start, width, half)

    pl.semaphore_wait(barrier, group - 1 + lines - 1)

    swaps = []
    for index, (start, width) in enumerate(spans):
        copy = pltpu.make_async_remote_copy(
            src_ref=outgoing.at[:, pl.ds(start, width)],
            dst_ref=panel.at[pl.ds(pl.multiple_of(tm * hours, hours), hours), pl.ds(start, width)],
            send_sem=swap_send.at[index],
            recv_sem=swap_recv.at[index],
            device_id=(space, 1 - tm),
            device_id_type=MESH,
        )
        copy.start()
        swaps.append(copy)

    for side in range(2):

        @pl.when(tm == side)
        def _():
            rows = slice(side * hours, (side + 1) * hours)
            for start, width in spans:
                place(panel, rows, x_ref, side * half, start, width, half)

    row = lax.broadcasted_iota(jnp.int32, (total, total), 0)
    col = lax.broadcasted_iota(jnp.int32, (total, total), 1)
    lagged = jnp.broadcast_to(coef_ref[...], (total, total))
    lagged = pltpu.roll(lagged, 1, axis=1, stride=1, stride_axis=0)
    turned = jnp.where(col > row, lagged, jnp.where(col == row, 1.0, 0.0))
    matrix = turned.T.astype(jnp.bfloat16)

    partial[...] = jnp.zeros_like(partial)
    for index, (start, width) in enumerate(spans):
        swaps[index].wait_recv()
        values = jnp.dot(
            matrix, panel[:, start : start + width], preferred_element_type=jnp.float32
        ).astype(jnp.bfloat16)
        filtered_ref[start : start + width, :] = values.T
        partial[...] += lax.dot_general(
            values, values, (((1,), (1,)), ((), ())), preferred_element_type=jnp.float32
        )

    copies = []
    for offset in range(1, group):
        other, device = in_group(offset)
        copy = pltpu.make_async_remote_copy(
            src_ref=partial.at[pl.ds(pl.multiple_of(other * share, share), share)],
            dst_ref=pieces.at[offset - 1],
            send_sem=rs_send.at[offset - 1],
            recv_sem=rs_recv.at[offset - 1],
            device_id=device,
            device_id_type=MESH,
        )
        copy.start()
        copies.append(copy)
    mine = pl.ds(pl.multiple_of(me * share, share), share)
    running = partial[mine, :]
    for offset in range(1, group):
        copies[offset - 1].wait_recv()
        running = running + pieces[offset - 1]
    reduced[...] = running
    planes[plane] = running

    for offset in range(1, lines):
        copy = pltpu.make_async_remote_copy(
            src_ref=reduced,
            dst_ref=planes.at[plane],
            send_sem=line_send.at[offset - 1],
            recv_sem=line_recv.at[offset - 1],
            device_id=in_line(offset),
            device_id_type=MESH,
        )
        copy.start()
        copies.append(copy)
    for offset in range(1, lines):
        copies[group - 1 + offset - 1].wait_recv()
    running = planes[0]
    for index in range(1, lines):
        running = running + planes[index]
    whole[mine, :] = running

    for offset in range(1, group):
        copy = pltpu.make_async_remote_copy(
            src_ref=whole.at[mine],
            dst_ref=whole.at[mine],
            send_sem=ag_send.at[offset - 1],
            recv_sem=ag_recv.at[offset - 1],
            device_id=in_group(offset)[1],
            device_id_type=MESH,
        )
        copy.start()
        copies.append(copy)
    for copy in copies[-(group - 1) :]:
        copy.wait_recv()
    gram_ref[...] = whole[...]
    for copy in swaps + copies:
        copy.wait_send()


def factor(gram_ref, store):
    size = gram_ref.shape[0]
    count = size // SUB
    full = (SUB, size)
    blocks = [gram_ref[SUB * b : SUB * (b + 1), :] for b in range(count)]
    lane = lax.broadcasted_iota(jnp.int32, full, 1)
    sub = lax.broadcasted_iota(jnp.int32, full, 0)
    for b in range(count):
        first = b * SUB
        inside = (lane >= first) & (lane < first + SUB)
        columns = [
            [jnp.broadcast_to(blocks[i][:, first + c : first + c + 1], full) for c in range(SUB)]
            for i in range(b, count)
        ]
        upper = [
            [
                jnp.broadcast_to(columns[0][c][r : r + 1, :], full) if c >= r else None
                for c in range(SUB)
            ]
            for r in range(SUB)
        ]
        rows = [
            jnp.where(
                inside,
                jnp.where(lane == first + r, 1.0, 0.0),
                jnp.broadcast_to(blocks[b][r : r + 1, :], full),
            )
            for r in range(SUB)
        ]
        unit = [[None] * SUB for _ in range(SUB)]
        inverse = [None] * SUB
        for c in range(SUB):
            inverse[c] = 1.0 / upper[c][c]
            for r in range(c + 1, SUB):
                unit[c][r] = upper[c][r] * inverse[c]
                for j in range(r, SUB):
                    upper[r][j] = upper[r][j] - unit[c][r] * upper[c][j]
                rows[r] = rows[r] - unit[c][r] * rows[c]
        store(b, rows, upper, lane, sub)
        solved = [rows[r] * inverse[r] for r in range(SUB)]
        for c in range(SUB - 1, 0, -1):
            for r in range(c):
                solved[r] = solved[r] - unit[r][c] * solved[c]
        for i in range(b + 1, count):
            terms = [columns[i - b][c] * solved[c] for c in range(SUB)]
            while len(terms) > 1:
                terms = [terms[t] + terms[t + 1] for t in range(0, len(terms), 2)]
            blocks[i] = jnp.where(inside, 0.0, blocks[i]) - terms[0]


def basis_kernel(points, gram_ref, filtered_ref, basis_ref, factor_ref, split, turned):
    size = gram_ref.shape[0]
    root = math.sqrt(points)

    def store(b, rows, upper, lane, sub):
        first = b * SUB
        block = rows[0]
        pivot = upper[0][0]
        for r in range(1, SUB):
            block = jnp.where(sub == r, rows[r], block)
            pivot = jnp.where(sub == r, upper[r][r], pivot)
        corner = block
        for r in range(SUB):
            for c in range(r, SUB):
                corner = jnp.where((sub == r) & (lane == first + c), upper[r][c], corner)
        diagonal = jnp.sqrt(pivot)
        here = slice(first, first + SUB)
        inverse = jnp.where(lane <= sub + first, block, 0.0) * (root / diagonal)
        top = inverse.astype(jnp.bfloat16).astype(jnp.float32)
        split[here, :] = top
        split[size + first : size + first + SUB, :] = inverse - top
        turned[here, :] = jnp.where(lane >= sub + first, corner, 0.0) / (diagonal * root)

    @pl.when(pl.program_id(0) == 0)
    def _():
        factor(gram_ref, store)
        factor_ref[...] = turned[...].T

    both = lax.dot_general(
        filtered_ref[...],
        split[...].astype(jnp.bfloat16),
        (((1,), (1,)), ((), ())),
        preferred_element_type=jnp.float32,
    )
    basis_ref[...] = both[:, :size] + both[:, size:]


def paired_body(thermal_anomaly, smoothing_coefs):
    hours, sites = thermal_anomaly.shape
    total = 2 * hours
    half = sites // 2
    tiles = pl.cdiv(half, LANES)
    step = pl.cdiv(tiles, CHUNKS)
    spans = [
        (t * LANES, min(step, tiles - t) * LANES) for t in range(0, tiles, step)
    ]
    padded = tiles * LANES
    group = PLANE * 2
    lines = lax.axis_size("space") // PLANE
    share = total // group
    dma = pltpu.SemaphoreType.DMA
    vmem = pl.BlockSpec(memory_space=pltpu.VMEM)
    filtered, gram = pl.pallas_call(
        functools.partial(gather_kernel, spans),
        out_shape=(
            jax.ShapeDtypeStruct((padded, total), jnp.bfloat16),
            jax.ShapeDtypeStruct((total, total), jnp.float32),
        ),
        in_specs=[vmem, vmem],
        out_specs=(vmem, vmem),
        scratch_shapes=[
            pltpu.VMEM((hours, padded), jnp.bfloat16),
            pltpu.VMEM((total, padded), jnp.bfloat16),
            pltpu.VMEM((total, total), jnp.float32),
            pltpu.VMEM((group - 1, share, total), jnp.float32),
            pltpu.VMEM((share, total), jnp.float32),
            pltpu.VMEM((lines, share, total), jnp.float32),
            pltpu.VMEM((total, total), jnp.float32),
            dma((len(spans),)),
            dma((len(spans),)),
            dma((group - 1,)),
            dma((group - 1,)),
            dma((lines - 1,)),
            dma((lines - 1,)),
            dma((group - 1,)),
            dma((group - 1,)),
        ],
        compiler_params=pltpu.CompilerParams(collective_id=0, has_side_effects=True),
        name="gather_gram",
    )(thermal_anomaly, smoothing_coefs[: total].reshape(1, total))

    width = step * LANES
    points = sites * lax.axis_size("space")
    basis, lower = pl.pallas_call(
        functools.partial(basis_kernel, points),
        grid=(pl.cdiv(half, width),),
        out_shape=(
            jax.ShapeDtypeStruct((half, total), jnp.float32),
            jax.ShapeDtypeStruct((total, total), jnp.float32),
        ),
        in_specs=[
            pl.BlockSpec((total, total), lambda i: (0, 0)),
            pl.BlockSpec((width, total), lambda i: (i, 0)),
        ],
        out_specs=(
            pl.BlockSpec((width, total), lambda i: (i, 0)),
            pl.BlockSpec((total, total), lambda i: (0, 0)),
        ),
        scratch_shapes=[
            pltpu.VMEM((2 * total, total), jnp.float32),
            pltpu.VMEM((total, total), jnp.float32),
        ],
        name="factor_basis",
    )(gram, filtered)
    return basis.T, lower


def body(thermal_anomaly, smoothing_coefs):
    hours, sites = thermal_anomaly.shape
    paired = (
        lax.axis_size("tm") == 2
        and 2 * hours == LANES
        and smoothing_coefs.shape[0] >= LANES
        and sites % 2 == 0
        and lax.axis_size("space") % PLANE == 0
        and lax.axis_size("space") > PLANE
    )
    return (paired_body if paired else general_body)(thermal_anomaly, smoothing_coefs)


def solution(mesh):
    placed = (P("tm", "space"), P())
    return jax.shard_map(
        body, mesh=mesh, in_specs=placed, out_specs=(P(None, ("space", "tm")), P()), check_vma=False
    )
```

```python
import functools
import math

import jax
import jax.numpy as jnp
from jax import lax
from jax.experimental import pallas as pl
from jax.experimental.pallas import tpu as pltpu
from jax.sharding import PartitionSpec as P

LANES = 128
SUB = 8
PLANE = 4
CHUNKS = 5
SLABS = 4
MESH = pl.DeviceIdType.MESH


def banded(coefficients, rows, cols, delay):
    lag = (
        lax.broadcasted_iota(jnp.int32, (rows, cols), 0)
        + delay
        - lax.broadcasted_iota(jnp.int32, (rows, cols), 1)
    )
    one_hot = lag[:, :, None] == lax.broadcasted_iota(
        jnp.int32, (1, 1, coefficients.shape[0]), 2
    )
    return jnp.sum(jnp.where(one_hot, coefficients.astype(jnp.float32), 0.0), axis=2).astype(
        coefficients.dtype
    )


def general_body(thermal_anomaly, smoothing_coefs):
    steps = thermal_anomaly.shape[0]
    blocks = lax.axis_size("tm")
    coefficients = jnp.concatenate([jnp.ones((1,), jnp.float32), smoothing_coefs]).astype(
        jnp.bfloat16
    )
    reach = min(blocks - 1, -(-(coefficients.shape[0] - 1) // steps))
    record = [thermal_anomaly]
    for distance in range(1, reach + 1):
        route = [(i, i + distance) for i in range(blocks - distance)]
        record.insert(0, lax.ppermute(thermal_anomaly, "tm", route))
    matrix = banded(coefficients, steps, (reach + 1) * steps, reach * steps)
    outgoing = jnp.dot(
        matrix, jnp.concatenate(record, axis=0), preferred_element_type=jnp.float32
    ).astype(jnp.bfloat16)
    arrived = lax.all_to_all(outgoing, "tm", split_axis=1, concat_axis=0, tiled=True)
    gram = lax.psum(
        jnp.dot(arrived, arrived.T, preferred_element_type=jnp.float32), ("space", "tm")
    )
    lower = jnp.linalg.cholesky(gram)
    rows = jax.scipy.linalg.solve_triangular(lower, arrived.astype(jnp.float32), lower=True)
    scale = jnp.sqrt(jnp.float32(thermal_anomaly.shape[1] * lax.axis_size("space")))
    return rows * scale, lower / scale


def place(dst, rows, x_ref, base, start, width, half):
    valid = min(width, half - start)
    low = base + start
    aligned = low // LANES * LANES
    shift = low - aligned
    end = min(aligned + pl.cdiv(shift + valid, LANES) * LANES, x_ref.shape[1])
    value = x_ref[:, aligned:end][:, shift : shift + valid]
    if valid < width:
        edge = valid // LANES * LANES
        dst[rows, start + edge : start + width] = jnp.zeros(
            (value.shape[0], width - edge), dst.dtype
        )
    dst[rows, start : start + valid] = value


def gather_kernel(
    spans,
    x_hbm,
    coef_hbm,
    filtered_hbm,
    gram_ref,
    x_ref,
    coef_ref,
    filtered_ref,
    load_sem,
    store_sem,
    outgoing,
    panel,
    partial,
    pieces,
    reduced,
    planes,
    whole,
    swap_send,
    swap_recv,
    rs_send,
    rs_recv,
    line_send,
    line_recv,
    ag_send,
    ag_recv,
):
    space = lax.axis_index("space")
    tm = lax.axis_index("tm")
    inner = space % PLANE
    plane = space // PLANE
    lines = lax.axis_size("space") // PLANE
    group = PLANE * 2
    me = inner * 2 + tm
    hours = x_ref.shape[0]
    total = 2 * hours
    half = x_ref.shape[1] // 2
    share = total // group

    def in_group(offset):
        other = (me + offset) % group
        return other, (plane * PLANE + other // 2, other % 2)

    def in_line(offset):
        return ((plane + offset) % lines * PLANE + inner, tm)

    barrier = pltpu.get_barrier_semaphore()
    for offset in range(1, group):
        pl.semaphore_signal(barrier, inc=1, device_id=in_group(offset)[1], device_id_type=MESH)
    for offset in range(1, lines):
        pl.semaphore_signal(barrier, inc=1, device_id=in_line(offset), device_id_type=MESH)

    slab = hours // SLABS
    loads = [
        pltpu.make_async_copy(
            x_hbm.at[pl.ds(slab * index, slab)],
            x_ref.at[pl.ds(slab * index, slab)],
            load_sem.at[index],
        )
        for index in range(SLABS)
    ] + [pltpu.make_async_copy(coef_hbm, coef_ref, load_sem.at[SLABS])]
    for copy in loads:
        copy.start()
    for copy in loads:
        copy.wait()

    swaps = []
    for index, (start, width) in enumerate(spans):
        for side in range(2):

            @pl.when(tm == side)
            def _():
                place(outgoing, slice(None), x_ref, (1 - side) * half, start, width, half)

        if index == 0:
            pl.semaphore_wait(barrier, group - 1 + lines - 1)
        copy = pltpu.make_async_remote_copy(
            src_ref=outgoing.at[:, pl.ds(start, width)],
            dst_ref=panel.at[pl.ds(pl.multiple_of(tm * hours, hours), hours), pl.ds(start, width)],
            send_sem=swap_send.at[index],
            recv_sem=swap_recv.at[index],
            device_id=(space, 1 - tm),
            device_id_type=MESH,
        )
        copy.start()
        swaps.append(copy)

    for side in range(2):

        @pl.when(tm == side)
        def _():
            rows = slice(side * hours, (side + 1) * hours)
            for start, width in spans:
                place(panel, rows, x_ref, side * half, start, width, half)

    row = lax.broadcasted_iota(jnp.int32, (total, total), 0)
    col = lax.broadcasted_iota(jnp.int32, (total, total), 1)
    lagged = jnp.broadcast_to(coef_ref[...], (total, total))
    lagged = pltpu.roll(lagged, 1, axis=1, stride=1, stride_axis=0)
    turned = jnp.where(col > row, lagged, jnp.where(col == row, 1.0, 0.0))
    matrix = turned.T.astype(jnp.bfloat16)

    stores = []
    partial[...] = jnp.zeros_like(partial)
    for index, (start, width) in enumerate(spans):
        swaps[index].wait_recv()
        values = jnp.dot(
            matrix, panel[:, start : start + width], preferred_element_type=jnp.float32
        ).astype(jnp.bfloat16)
        filtered_ref[start : start + width, :] = values.T
        store = pltpu.make_async_copy(
            filtered_ref.at[pl.ds(start, width)],
            filtered_hbm.at[pl.ds(start, width)],
            store_sem.at[index],
        )
        store.start()
        stores.append(store)
        partial[...] += lax.dot_general(
            values, values, (((1,), (1,)), ((), ())), preferred_element_type=jnp.float32
        )

    copies = []
    for offset in range(1, group):
        other, device = in_group(offset)
        copy = pltpu.make_async_remote_copy(
            src_ref=partial.at[pl.ds(pl.multiple_of(other * share, share), share)],
            dst_ref=pieces.at[offset - 1],
            send_sem=rs_send.at[offset - 1],
            recv_sem=rs_recv.at[offset - 1],
            device_id=device,
            device_id_type=MESH,
        )
        copy.start()
        copies.append(copy)
    mine = pl.ds(pl.multiple_of(me * share, share), share)
    running = partial[mine, :]
    for offset in range(1, group):
        copies[offset - 1].wait_recv()
        running = running + pieces[offset - 1]
    reduced[...] = running
    planes[plane] = running

    for offset in range(1, lines):
        copy = pltpu.make_async_remote_copy(
            src_ref=reduced,
            dst_ref=planes.at[plane],
            send_sem=line_send.at[offset - 1],
            recv_sem=line_recv.at[offset - 1],
            device_id=in_line(offset),
            device_id_type=MESH,
        )
        copy.start()
        copies.append(copy)
    for offset in range(1, lines):
        copies[group - 1 + offset - 1].wait_recv()
    running = planes[0]
    for index in range(1, lines):
        running = running + planes[index]
    whole[mine, :] = running

    for offset in range(1, group):
        copy = pltpu.make_async_remote_copy(
            src_ref=whole.at[mine],
            dst_ref=whole.at[mine],
            send_sem=ag_send.at[offset - 1],
            recv_sem=ag_recv.at[offset - 1],
            device_id=in_group(offset)[1],
            device_id_type=MESH,
        )
        copy.start()
        copies.append(copy)
    for copy in copies[-(group - 1) :]:
        copy.wait_recv()
    gram_ref[...] = whole[...]
    for copy in swaps + copies:
        copy.wait_send()
    for store in stores:
        store.wait()


def factor(gram_ref, store):
    size = gram_ref.shape[0]
    count = size // SUB
    full = (SUB, size)
    blocks = [gram_ref[SUB * b : SUB * (b + 1), :] for b in range(count)]
    lane = lax.broadcasted_iota(jnp.int32, full, 1)
    sub = lax.broadcasted_iota(jnp.int32, full, 0)
    for b in range(count):
        first = b * SUB
        inside = (lane >= first) & (lane < first + SUB)
        columns = [
            [jnp.broadcast_to(blocks[i][:, first + c : first + c + 1], full) for c in range(SUB)]
            for i in range(b, count)
        ]
        upper = [
            [
                jnp.broadcast_to(columns[0][c][r : r + 1, :], full) if c >= r else None
                for c in range(SUB)
            ]
            for r in range(SUB)
        ]
        rows = [
            jnp.where(
                inside,
                jnp.where(lane == first + r, 1.0, 0.0),
                jnp.broadcast_to(blocks[b][r : r + 1, :], full),
            )
            for r in range(SUB)
        ]
        unit = [[None] * SUB for _ in range(SUB)]
        inverse = [None] * SUB
        for c in range(SUB):
            inverse[c] = 1.0 / upper[c][c]
            for r in range(c + 1, SUB):
                unit[c][r] = upper[c][r] * inverse[c]
                for j in range(r, SUB):
                    upper[r][j] = upper[r][j] - unit[c][r] * upper[c][j]
                rows[r] = rows[r] - unit[c][r] * rows[c]
        store(b, rows, upper, lane, sub)
        solved = [rows[r] * inverse[r] for r in range(SUB)]
        for c in range(SUB - 1, 0, -1):
            for r in range(c):
                solved[r] = solved[r] - unit[r][c] * solved[c]
        for i in range(b + 1, count):
            terms = [columns[i - b][c] * solved[c] for c in range(SUB)]
            while len(terms) > 1:
                terms = [terms[t] + terms[t + 1] for t in range(0, len(terms), 2)]
            blocks[i] = jnp.where(inside, 0.0, blocks[i]) - terms[0]


def basis_kernel(points, gram_ref, filtered_ref, basis_ref, factor_ref, split, turned):
    size = gram_ref.shape[0]
    root = math.sqrt(points)

    def store(b, rows, upper, lane, sub):
        first = b * SUB
        block = rows[0]
        pivot = upper[0][0]
        for r in range(1, SUB):
            block = jnp.where(sub == r, rows[r], block)
            pivot = jnp.where(sub == r, upper[r][r], pivot)
        corner = block
        for r in range(SUB):
            for c in range(r, SUB):
                corner = jnp.where((sub == r) & (lane == first + c), upper[r][c], corner)
        diagonal = jnp.sqrt(pivot)
        here = slice(first, first + SUB)
        inverse = jnp.where(lane <= sub + first, block, 0.0) * (root / diagonal)
        top = inverse.astype(jnp.bfloat16).astype(jnp.float32)
        split[here, :] = top
        split[size + first : size + first + SUB, :] = inverse - top
        turned[here, :] = jnp.where(lane >= sub + first, corner, 0.0) / (diagonal * root)

    @pl.when(pl.program_id(0) == 0)
    def _():
        factor(gram_ref, store)
        factor_ref[...] = turned[...].T

    both = lax.dot_general(
        filtered_ref[...],
        split[...].astype(jnp.bfloat16),
        (((1,), (1,)), ((), ())),
        preferred_element_type=jnp.float32,
    )
    basis_ref[...] = both[:, :size] + both[:, size:]


def paired_body(thermal_anomaly, smoothing_coefs):
    hours, sites = thermal_anomaly.shape
    total = 2 * hours
    half = sites // 2
    tiles = pl.cdiv(half, LANES)
    step = pl.cdiv(tiles, CHUNKS)
    spans = [
        (t * LANES, min(step, tiles - t) * LANES) for t in range(0, tiles, step)
    ]
    padded = tiles * LANES
    group = PLANE * 2
    lines = lax.axis_size("space") // PLANE
    share = total // group
    dma = pltpu.SemaphoreType.DMA
    vmem = pl.BlockSpec(memory_space=pltpu.VMEM)
    anywhere = pl.BlockSpec(memory_space=pl.ANY)
    filtered, gram = pl.pallas_call(
        functools.partial(gather_kernel, spans),
        out_shape=(
            jax.ShapeDtypeStruct((padded, total), jnp.bfloat16),
            jax.ShapeDtypeStruct((total, total), jnp.float32),
        ),
        in_specs=[anywhere, anywhere],
        out_specs=(anywhere, vmem),
        scratch_shapes=[
            pltpu.VMEM((hours, sites), jnp.bfloat16),
            pltpu.VMEM((1, total), jnp.float32),
            pltpu.VMEM((padded, total), jnp.bfloat16),
            dma((SLABS + 1,)),
            dma((len(spans),)),
            pltpu.VMEM((hours, padded), jnp.bfloat16),
            pltpu.VMEM((total, padded), jnp.bfloat16),
            pltpu.VMEM((total, total), jnp.float32),
            pltpu.VMEM((group - 1, share, total), jnp.float32),
            pltpu.VMEM((share, total), jnp.float32),
            pltpu.VMEM((lines, share, total), jnp.float32),
            pltpu.VMEM((total, total), jnp.float32),
            dma((len(spans),)),
            dma((len(spans),)),
            dma((group - 1,)),
            dma((group - 1,)),
            dma((lines - 1,)),
            dma((lines - 1,)),
            dma((group - 1,)),
            dma((group - 1,)),
        ],
        compiler_params=pltpu.CompilerParams(collective_id=0, has_side_effects=True),
        name="gather_gram",
    )(thermal_anomaly, smoothing_coefs[: total].reshape(1, total))

    width = step * LANES
    points = sites * lax.axis_size("space")
    basis, lower = pl.pallas_call(
        functools.partial(basis_kernel, points),
        grid=(pl.cdiv(half, width),),
        out_shape=(
            jax.ShapeDtypeStruct((half, total), jnp.float32),
            jax.ShapeDtypeStruct((total, total), jnp.float32),
        ),
        in_specs=[
            pl.BlockSpec((total, total), lambda i: (0, 0)),
            pl.BlockSpec((width, total), lambda i: (i, 0)),
        ],
        out_specs=(
            pl.BlockSpec((width, total), lambda i: (i, 0)),
            pl.BlockSpec((total, total), lambda i: (0, 0)),
        ),
        scratch_shapes=[
            pltpu.VMEM((2 * total, total), jnp.float32),
            pltpu.VMEM((total, total), jnp.float32),
        ],
        name="factor_basis",
    )(gram, filtered)
    return basis.T, lower


def body(thermal_anomaly, smoothing_coefs):
    hours, sites = thermal_anomaly.shape
    paired = (
        lax.axis_size("tm") == 2
        and 2 * hours == LANES
        and smoothing_coefs.shape[0] >= LANES
        and sites % 2 == 0
        and lax.axis_size("space") % PLANE == 0
        and lax.axis_size("space") > PLANE
    )
    return (paired_body if paired else general_body)(thermal_anomaly, smoothing_coefs)


def solution(mesh):
    placed = (P("tm", "space"), P())
    return jax.shard_map(
        body, mesh=mesh, in_specs=placed, out_specs=(P(None, ("space", "tm")), P()), check_vma=False
    )
```

```python
import functools
import math

import jax
import jax.numpy as jnp
from jax import lax
from jax.experimental import pallas as pl
from jax.experimental.pallas import tpu as pltpu
from jax.sharding import PartitionSpec as P

LANES = 128
SUB = 8
PLANE = 4
CHUNKS = 5
SLABS = 4
MESH = pl.DeviceIdType.MESH


def banded(coefficients, rows, cols, delay):
    lag = (
        lax.broadcasted_iota(jnp.int32, (rows, cols), 0)
        + delay
        - lax.broadcasted_iota(jnp.int32, (rows, cols), 1)
    )
    one_hot = lag[:, :, None] == lax.broadcasted_iota(
        jnp.int32, (1, 1, coefficients.shape[0]), 2
    )
    return jnp.sum(jnp.where(one_hot, coefficients.astype(jnp.float32), 0.0), axis=2).astype(
        coefficients.dtype
    )


def general_body(thermal_anomaly, smoothing_coefs):
    steps = thermal_anomaly.shape[0]
    blocks = lax.axis_size("tm")
    coefficients = jnp.concatenate([jnp.ones((1,), jnp.float32), smoothing_coefs]).astype(
        jnp.bfloat16
    )
    reach = min(blocks - 1, -(-(coefficients.shape[0] - 1) // steps))
    record = [thermal_anomaly]
    for distance in range(1, reach + 1):
        route = [(i, i + distance) for i in range(blocks - distance)]
        record.insert(0, lax.ppermute(thermal_anomaly, "tm", route))
    matrix = banded(coefficients, steps, (reach + 1) * steps, reach * steps)
    outgoing = jnp.dot(
        matrix, jnp.concatenate(record, axis=0), preferred_element_type=jnp.float32
    ).astype(jnp.bfloat16)
    arrived = lax.all_to_all(outgoing, "tm", split_axis=1, concat_axis=0, tiled=True)
    gram = lax.psum(
        jnp.dot(arrived, arrived.T, preferred_element_type=jnp.float32), ("space", "tm")
    )
    lower = jnp.linalg.cholesky(gram)
    rows = jax.scipy.linalg.solve_triangular(lower, arrived.astype(jnp.float32), lower=True)
    scale = jnp.sqrt(jnp.float32(thermal_anomaly.shape[1] * lax.axis_size("space")))
    return rows * scale, lower / scale


def place(dst, rows, x_ref, base, start, width, half):
    valid = min(width, half - start)
    low = base + start
    aligned = low // LANES * LANES
    shift = low - aligned
    end = min(aligned + pl.cdiv(shift + valid, LANES) * LANES, x_ref.shape[1])
    value = x_ref[:, aligned:end][:, shift : shift + valid]
    if valid < width:
        edge = valid // LANES * LANES
        dst[rows, start + edge : start + width] = jnp.zeros(
            (value.shape[0], width - edge), dst.dtype
        )
    dst[rows, start : start + valid] = value


def gather_kernel(
    spans,
    x_hbm,
    coef_hbm,
    filtered_hbm,
    gram_ref,
    x_ref,
    coef_ref,
    filtered_ref,
    load_sem,
    store_sem,
    outgoing,
    panel,
    partial,
    pieces,
    reduced,
    planes,
    whole,
    swap_send,
    swap_recv,
    rs_send,
    rs_recv,
    line_send,
    line_recv,
    ag_send,
    ag_recv,
):
    space = lax.axis_index("space")
    tm = lax.axis_index("tm")
    inner = space % PLANE
    plane = space // PLANE
    lines = lax.axis_size("space") // PLANE
    group = PLANE * 2
    me = inner * 2 + tm
    hours = x_ref.shape[0]
    total = 2 * hours
    half = x_ref.shape[1] // 2
    share = total // group

    def in_group(offset):
        other = (me + offset) % group
        return other, (plane * PLANE + other // 2, other % 2)

    def in_line(offset):
        return ((plane + offset) % lines * PLANE + inner, tm)

    barrier = pltpu.get_barrier_semaphore()
    for offset in range(1, group):
        pl.semaphore_signal(barrier, inc=1, device_id=in_group(offset)[1], device_id_type=MESH)
    for offset in range(1, lines):
        pl.semaphore_signal(barrier, inc=1, device_id=in_line(offset), device_id_type=MESH)

    slab = hours // SLABS
    loads = [
        pltpu.make_async_copy(
            x_hbm.at[pl.ds(slab * index, slab)],
            x_ref.at[pl.ds(slab * index, slab)],
            load_sem.at[index],
        )
        for index in range(SLABS)
    ] + [pltpu.make_async_copy(coef_hbm, coef_ref, load_sem.at[SLABS])]
    for copy in loads:
        copy.start()
    for copy in loads:
        copy.wait()

    swaps = []
    for index, (start, width) in enumerate(spans):
        for side in range(2):

            @pl.when(tm == side)
            def _():
                place(outgoing, slice(None), x_ref, (1 - side) * half, start, width, half)

        if index == 0:
            pl.semaphore_wait(barrier, group - 1 + lines - 1)
        copy = pltpu.make_async_remote_copy(
            src_ref=outgoing.at[:, pl.ds(start, width)],
            dst_ref=panel.at[pl.ds(pl.multiple_of(tm * hours, hours), hours), pl.ds(start, width)],
            send_sem=swap_send.at[index],
            recv_sem=swap_recv.at[index],
            device_id=(space, 1 - tm),
            device_id_type=MESH,
        )
        copy.start()
        swaps.append(copy)

    for side in range(2):

        @pl.when(tm == side)
        def _():
            rows = slice(side * hours, (side + 1) * hours)
            for start, width in spans:
                place(panel, rows, x_ref, side * half, start, width, half)

    row = lax.broadcasted_iota(jnp.int32, (total, total), 0)
    col = lax.broadcasted_iota(jnp.int32, (total, total), 1)
    lagged = jnp.broadcast_to(coef_ref[...], (total, total))
    lagged = pltpu.roll(lagged, 1, axis=1, stride=1, stride_axis=0)
    turned = jnp.where(col > row, lagged, jnp.where(col == row, 1.0, 0.0))
    matrix = turned.T.astype(jnp.bfloat16)

    stores = []
    partial[...] = jnp.zeros_like(partial)
    for index, (start, width) in enumerate(spans):
        swaps[index].wait_recv()
        values = jnp.dot(
            matrix, panel[:, start : start + width], preferred_element_type=jnp.float32
        ).astype(jnp.bfloat16)
        filtered_ref[start : start + width, :] = values.T
        store = pltpu.make_async_copy(
            filtered_ref.at[pl.ds(start, width)],
            filtered_hbm.at[pl.ds(start, width)],
            store_sem.at[index],
        )
        store.start()
        stores.append(store)
        partial[...] += lax.dot_general(
            values, values, (((1,), (1,)), ((), ())), preferred_element_type=jnp.float32
        )

    copies = []
    for offset in range(1, group):
        other, device = in_group(offset)
        copy = pltpu.make_async_remote_copy(
            src_ref=partial.at[pl.ds(pl.multiple_of(other * share, share), share)],
            dst_ref=pieces.at[offset - 1],
            send_sem=rs_send.at[offset - 1],
            recv_sem=rs_recv.at[offset - 1],
            device_id=device,
            device_id_type=MESH,
        )
        copy.start()
        copies.append(copy)
    mine = pl.ds(pl.multiple_of(me * share, share), share)
    running = partial[mine, :]
    for offset in range(1, group):
        copies[offset - 1].wait_recv()
        running = running + pieces[offset - 1]
    reduced[...] = running
    planes[plane] = running

    for offset in range(1, lines):
        copy = pltpu.make_async_remote_copy(
            src_ref=reduced,
            dst_ref=planes.at[plane],
            send_sem=line_send.at[offset - 1],
            recv_sem=line_recv.at[offset - 1],
            device_id=in_line(offset),
            device_id_type=MESH,
        )
        copy.start()
        copies.append(copy)
    for offset in range(1, lines):
        copies[group - 1 + offset - 1].wait_recv()
    running = planes[0]
    for index in range(1, lines):
        running = running + planes[index]
    whole[mine, :] = running

    for offset in range(1, group):
        copy = pltpu.make_async_remote_copy(
            src_ref=whole.at[mine],
            dst_ref=whole.at[mine],
            send_sem=ag_send.at[offset - 1],
            recv_sem=ag_recv.at[offset - 1],
            device_id=in_group(offset)[1],
            device_id_type=MESH,
        )
        copy.start()
        copies.append(copy)
    for copy in copies[-(group - 1) :]:
        copy.wait_recv()
    gram_ref[...] = whole[...]
    for copy in swaps + copies:
        copy.wait_send()
    for store in stores:
        store.wait()


def factor(gram_ref, store):
    size = gram_ref.shape[0]
    count = size // SUB
    full = (SUB, size)
    blocks = [gram_ref[SUB * b : SUB * (b + 1), :] for b in range(count)]
    lane = lax.broadcasted_iota(jnp.int32, full, 1)
    sub = lax.broadcasted_iota(jnp.int32, full, 0)
    for b in range(count):
        first = b * SUB
        inside = (lane >= first) & (lane < first + SUB)
        columns = [
            [jnp.broadcast_to(blocks[i][:, first + c : first + c + 1], full) for c in range(SUB)]
            for i in range(b, count)
        ]
        upper = [
            [
                jnp.broadcast_to(columns[0][c][r : r + 1, :], full) if c >= r else None
                for c in range(SUB)
            ]
            for r in range(SUB)
        ]
        rows = [
            jnp.where(
                inside,
                jnp.where(lane == first + r, 1.0, 0.0),
                jnp.broadcast_to(blocks[b][r : r + 1, :], full),
            )
            for r in range(SUB)
        ]
        unit = [[None] * SUB for _ in range(SUB)]
        inverse = [None] * SUB
        for c in range(SUB):
            inverse[c] = 1.0 / upper[c][c]
            for r in range(c + 1, SUB):
                unit[c][r] = upper[c][r] * inverse[c]
                for j in range(r, SUB):
                    upper[r][j] = upper[r][j] - unit[c][r] * upper[c][j]
                rows[r] = rows[r] - unit[c][r] * rows[c]
        store(b, rows, upper, lane, sub)
        solved = [rows[r] * inverse[r] for r in range(SUB)]
        for c in range(SUB - 1, 0, -1):
            for r in range(c):
                solved[r] = solved[r] - unit[r][c] * solved[c]
        for i in range(b + 1, count):
            terms = [columns[i - b][c] * solved[c] for c in range(SUB)]
            while len(terms) > 1:
                terms = [terms[t] + terms[t + 1] for t in range(0, len(terms), 2)]
            blocks[i] = jnp.where(inside, 0.0, blocks[i]) - terms[0]


def basis_kernel(
    points,
    spans,
    gram_ref,
    filtered_hbm,
    basis_hbm,
    factor_hbm,
    filtered_ref,
    basis_ref,
    factor_ref,
    split,
    turned,
    load_sem,
    store_sem,
):
    size = gram_ref.shape[0]
    load = pltpu.make_async_copy(filtered_hbm, filtered_ref, load_sem)
    load.start()
    root = math.sqrt(points)

    def store(b, rows, upper, lane, sub):
        first = b * SUB
        block = rows[0]
        pivot = upper[0][0]
        for r in range(1, SUB):
            block = jnp.where(sub == r, rows[r], block)
            pivot = jnp.where(sub == r, upper[r][r], pivot)
        corner = block
        for r in range(SUB):
            for c in range(r, SUB):
                corner = jnp.where((sub == r) & (lane == first + c), upper[r][c], corner)
        diagonal = jnp.sqrt(pivot)
        here = slice(first, first + SUB)
        inverse = jnp.where(lane <= sub + first, block, 0.0) * (root / diagonal)
        top = inverse.astype(jnp.bfloat16).astype(jnp.float32)
        split[here, :] = top
        split[size + first : size + first + SUB, :] = inverse - top
        turned[here, :] = jnp.where(lane >= sub + first, corner, 0.0) / (diagonal * root)

    factor(gram_ref, store)
    load.wait()
    both_parts = split[...].astype(jnp.bfloat16)
    stores = []
    for index, (start, width) in enumerate(spans):
        rows = pl.ds(start, min(width, basis_ref.shape[0] - start))
        both = lax.dot_general(
            filtered_ref[rows, :],
            both_parts,
            (((1,), (1,)), ((), ())),
            preferred_element_type=jnp.float32,
        )
        basis_ref[rows, :] = both[:, :size] + both[:, size:]
        copy = pltpu.make_async_copy(
            basis_ref.at[rows], basis_hbm.at[rows], store_sem.at[index]
        )
        copy.start()
        stores.append(copy)
        if index == 0:
            factor_ref[...] = turned[...].T
            copy = pltpu.make_async_copy(factor_ref, factor_hbm, store_sem.at[len(spans)])
            copy.start()
            stores.append(copy)
    for copy in stores:
        copy.wait()


def paired_body(thermal_anomaly, smoothing_coefs):
    hours, sites = thermal_anomaly.shape
    total = 2 * hours
    half = sites // 2
    tiles = pl.cdiv(half, LANES)
    edge = max(1, tiles // (2 * CHUNKS))
    step = max(1, pl.cdiv(tiles - 2 * edge, CHUNKS - 2))
    cuts = [0, *range(edge, max(edge, tiles - edge), step), max(edge, tiles - edge), tiles]
    spans = [(a * LANES, (b - a) * LANES) for a, b in zip(cuts, cuts[1:]) if b > a]
    padded = tiles * LANES
    group = PLANE * 2
    lines = lax.axis_size("space") // PLANE
    share = total // group
    dma = pltpu.SemaphoreType.DMA
    vmem = pl.BlockSpec(memory_space=pltpu.VMEM)
    anywhere = pl.BlockSpec(memory_space=pl.ANY)
    filtered, gram = pl.pallas_call(
        functools.partial(gather_kernel, spans),
        out_shape=(
            jax.ShapeDtypeStruct((padded, total), jnp.bfloat16),
            jax.ShapeDtypeStruct((total, total), jnp.float32),
        ),
        in_specs=[anywhere, anywhere],
        out_specs=(anywhere, vmem),
        scratch_shapes=[
            pltpu.VMEM((hours, sites), jnp.bfloat16),
            pltpu.VMEM((1, total), jnp.float32),
            pltpu.VMEM((padded, total), jnp.bfloat16),
            dma((SLABS + 1,)),
            dma((len(spans),)),
            pltpu.VMEM((hours, padded), jnp.bfloat16),
            pltpu.VMEM((total, padded), jnp.bfloat16),
            pltpu.VMEM((total, total), jnp.float32),
            pltpu.VMEM((group - 1, share, total), jnp.float32),
            pltpu.VMEM((share, total), jnp.float32),
            pltpu.VMEM((lines, share, total), jnp.float32),
            pltpu.VMEM((total, total), jnp.float32),
            dma((len(spans),)),
            dma((len(spans),)),
            dma((group - 1,)),
            dma((group - 1,)),
            dma((lines - 1,)),
            dma((lines - 1,)),
            dma((group - 1,)),
            dma((group - 1,)),
        ],
        compiler_params=pltpu.CompilerParams(collective_id=0, has_side_effects=True),
        name="gather_gram",
    )(thermal_anomaly, smoothing_coefs[: total].reshape(1, total))

    points = sites * lax.axis_size("space")
    basis, lower = pl.pallas_call(
        functools.partial(basis_kernel, points, spans),
        out_shape=(
            jax.ShapeDtypeStruct((half, total), jnp.float32),
            jax.ShapeDtypeStruct((total, total), jnp.float32),
        ),
        in_specs=[vmem, anywhere],
        out_specs=(anywhere, anywhere),
        scratch_shapes=[
            pltpu.VMEM((padded, total), jnp.bfloat16),
            pltpu.VMEM((half, total), jnp.float32),
            pltpu.VMEM((total, total), jnp.float32),
            pltpu.VMEM((2 * total, total), jnp.float32),
            pltpu.VMEM((total, total), jnp.float32),
            dma,
            dma((len(spans) + 1,)),
        ],
        name="factor_basis",
    )(gram, filtered)
    return basis.T, lower


def body(thermal_anomaly, smoothing_coefs):
    hours, sites = thermal_anomaly.shape
    paired = (
        lax.axis_size("tm") == 2
        and 2 * hours == LANES
        and smoothing_coefs.shape[0] >= LANES
        and sites % 2 == 0
        and lax.axis_size("space") % PLANE == 0
        and lax.axis_size("space") > PLANE
    )
    return (paired_body if paired else general_body)(thermal_anomaly, smoothing_coefs)


def solution(mesh):
    placed = (P("tm", "space"), P())
    return jax.shard_map(
        body, mesh=mesh, in_specs=placed, out_specs=(P(None, ("space", "tm")), P()), check_vma=False
    )
```

```python
import functools
import math

import jax
import jax.numpy as jnp
from jax import lax
from jax.experimental import pallas as pl
from jax.experimental.pallas import tpu as pltpu
from jax.sharding import PartitionSpec as P

LANES = 128
SUB = 8
PLANE = 4
CHUNKS = 5
SLABS = 4
GRANT = 16 * 2**20
MESH = pl.DeviceIdType.MESH


def banded(coefficients, rows, cols, delay):
    lag = (
        lax.broadcasted_iota(jnp.int32, (rows, cols), 0)
        + delay
        - lax.broadcasted_iota(jnp.int32, (rows, cols), 1)
    )
    one_hot = lag[:, :, None] == lax.broadcasted_iota(
        jnp.int32, (1, 1, coefficients.shape[0]), 2
    )
    return jnp.sum(jnp.where(one_hot, coefficients.astype(jnp.float32), 0.0), axis=2).astype(
        coefficients.dtype
    )


def general_body(thermal_anomaly, smoothing_coefs):
    steps = thermal_anomaly.shape[0]
    blocks = lax.axis_size("tm")
    coefficients = jnp.concatenate([jnp.ones((1,), jnp.float32), smoothing_coefs]).astype(
        jnp.bfloat16
    )
    reach = min(blocks - 1, -(-(coefficients.shape[0] - 1) // steps))
    record = [thermal_anomaly]
    for distance in range(1, reach + 1):
        route = [(i, i + distance) for i in range(blocks - distance)]
        record.insert(0, lax.ppermute(thermal_anomaly, "tm", route))
    matrix = banded(coefficients, steps, (reach + 1) * steps, reach * steps)
    outgoing = jnp.dot(
        matrix, jnp.concatenate(record, axis=0), preferred_element_type=jnp.float32
    ).astype(jnp.bfloat16)
    arrived = lax.all_to_all(outgoing, "tm", split_axis=1, concat_axis=0, tiled=True)
    gram = lax.psum(
        jnp.dot(arrived, arrived.T, preferred_element_type=jnp.float32), ("space", "tm")
    )
    lower = jnp.linalg.cholesky(gram)
    rows = jax.scipy.linalg.solve_triangular(lower, arrived.astype(jnp.float32), lower=True)
    scale = jnp.sqrt(jnp.float32(thermal_anomaly.shape[1] * lax.axis_size("space")))
    return rows * scale, lower / scale


def place(dst, rows, x_ref, base, start, width, half):
    valid = min(width, half - start)
    low = base + start
    aligned = low // LANES * LANES
    shift = low - aligned
    end = min(aligned + pl.cdiv(shift + valid, LANES) * LANES, x_ref.shape[1])
    value = x_ref[:, aligned:end][:, shift : shift + valid]
    if valid < width:
        edge = valid // LANES * LANES
        dst[rows, start + edge : start + width] = jnp.zeros(
            (value.shape[0], width - edge), dst.dtype
        )
    dst[rows, start : start + valid] = value


def gather_kernel(
    spans,
    x_hbm,
    coef_hbm,
    filtered_hbm,
    gram_ref,
    x_ref,
    coef_ref,
    filtered_ref,
    load_sem,
    store_sem,
    outgoing,
    panel,
    partial,
    pieces,
    reduced,
    planes,
    whole,
    swap_send,
    swap_recv,
    rs_send,
    rs_recv,
    line_send,
    line_recv,
    ag_send,
    ag_recv,
):
    space = lax.axis_index("space")
    tm = lax.axis_index("tm")
    inner = space % PLANE
    plane = space // PLANE
    lines = lax.axis_size("space") // PLANE
    group = PLANE * 2
    me = inner * 2 + tm
    hours = x_ref.shape[0]
    total = 2 * hours
    half = x_ref.shape[1] // 2
    share = total // group

    def in_group(offset):
        other = (me + offset) % group
        return other, (plane * PLANE + other // 2, other % 2)

    def in_line(offset):
        return ((plane + offset) % lines * PLANE + inner, tm)

    barrier = pltpu.get_barrier_semaphore()
    for offset in range(1, group):
        pl.semaphore_signal(barrier, inc=1, device_id=in_group(offset)[1], device_id_type=MESH)
    for offset in range(1, lines):
        pl.semaphore_signal(barrier, inc=1, device_id=in_line(offset), device_id_type=MESH)

    slab = hours // SLABS
    loads = [
        pltpu.make_async_copy(
            x_hbm.at[pl.ds(slab * index, slab)],
            x_ref.at[pl.ds(slab * index, slab)],
            load_sem.at[index],
        )
        for index in range(SLABS)
    ] + [pltpu.make_async_copy(coef_hbm, coef_ref, load_sem.at[SLABS])]
    for copy in loads:
        copy.start()
    for copy in loads:
        copy.wait()

    swaps = []
    for index, (start, width) in enumerate(spans):
        for side in range(2):

            @pl.when(tm == side)
            def _():
                place(outgoing, slice(None), x_ref, (1 - side) * half, start, width, half)

        if index == 0:
            pl.semaphore_wait(barrier, group - 1 + lines - 1)
        copy = pltpu.make_async_remote_copy(
            src_ref=outgoing.at[:, pl.ds(start, width)],
            dst_ref=panel.at[pl.ds(pl.multiple_of(tm * hours, hours), hours), pl.ds(start, width)],
            send_sem=swap_send.at[index],
            recv_sem=swap_recv.at[index],
            device_id=(space, 1 - tm),
            device_id_type=MESH,
        )
        copy.start()
        swaps.append(copy)

    for side in range(2):

        @pl.when(tm == side)
        def _():
            rows = slice(side * hours, (side + 1) * hours)
            for start, width in spans:
                place(panel, rows, x_ref, side * half, start, width, half)

    row = lax.broadcasted_iota(jnp.int32, (total, total), 0)
    col = lax.broadcasted_iota(jnp.int32, (total, total), 1)
    lagged = jnp.broadcast_to(coef_ref[...], (total, total))
    lagged = pltpu.roll(lagged, 1, axis=1, stride=1, stride_axis=0)
    turned = jnp.where(col > row, lagged, jnp.where(col == row, 1.0, 0.0))
    matrix = turned.T.astype(jnp.bfloat16)

    stores = []
    partial[...] = jnp.zeros_like(partial)
    for index, (start, width) in enumerate(spans):
        swaps[index].wait_recv()
        values = jnp.dot(
            matrix, panel[:, start : start + width], preferred_element_type=jnp.float32
        ).astype(jnp.bfloat16)
        filtered_ref[start : start + width, :] = values.T
        store = pltpu.make_async_copy(
            filtered_ref.at[pl.ds(start, width)],
            filtered_hbm.at[pl.ds(start, width)],
            store_sem.at[index],
        )
        store.start()
        stores.append(store)
        partial[...] += lax.dot_general(
            values, values, (((1,), (1,)), ((), ())), preferred_element_type=jnp.float32
        )

    copies = []
    for offset in range(1, group):
        other, device = in_group(offset)
        copy = pltpu.make_async_remote_copy(
            src_ref=partial.at[pl.ds(pl.multiple_of(other * share, share), share)],
            dst_ref=pieces.at[offset - 1],
            send_sem=rs_send.at[offset - 1],
            recv_sem=rs_recv.at[offset - 1],
            device_id=device,
            device_id_type=MESH,
        )
        copy.start()
        copies.append(copy)
    mine = pl.ds(pl.multiple_of(me * share, share), share)
    running = partial[mine, :]
    for offset in range(1, group):
        copies[offset - 1].wait_recv()
        running = running + pieces[offset - 1]
    reduced[...] = running
    planes[plane] = running

    for offset in range(1, lines):
        copy = pltpu.make_async_remote_copy(
            src_ref=reduced,
            dst_ref=planes.at[plane],
            send_sem=line_send.at[offset - 1],
            recv_sem=line_recv.at[offset - 1],
            device_id=in_line(offset),
            device_id_type=MESH,
        )
        copy.start()
        copies.append(copy)
    for offset in range(1, lines):
        copies[group - 1 + offset - 1].wait_recv()
    running = planes[0]
    for index in range(1, lines):
        running = running + planes[index]
    whole[mine, :] = running

    for offset in range(1, group):
        copy = pltpu.make_async_remote_copy(
            src_ref=whole.at[mine],
            dst_ref=whole.at[mine],
            send_sem=ag_send.at[offset - 1],
            recv_sem=ag_recv.at[offset - 1],
            device_id=in_group(offset)[1],
            device_id_type=MESH,
        )
        copy.start()
        copies.append(copy)
    for copy in copies[-(group - 1) :]:
        copy.wait_recv()
    gram_ref[...] = whole[...]
    for copy in swaps + copies:
        copy.wait_send()
    for store in stores:
        store.wait()


def factor(gram_ref, store):
    size = gram_ref.shape[0]
    count = size // SUB
    full = (SUB, size)
    blocks = [gram_ref[SUB * b : SUB * (b + 1), :] for b in range(count)]
    lane = lax.broadcasted_iota(jnp.int32, full, 1)
    sub = lax.broadcasted_iota(jnp.int32, full, 0)
    for b in range(count):
        first = b * SUB
        inside = (lane >= first) & (lane < first + SUB)
        columns = [
            [jnp.broadcast_to(blocks[i][:, first + c : first + c + 1], full) for c in range(SUB)]
            for i in range(b, count)
        ]
        upper = [
            [
                jnp.broadcast_to(columns[0][c][r : r + 1, :], full) if c >= r else None
                for c in range(SUB)
            ]
            for r in range(SUB)
        ]
        rows = [
            jnp.where(
                inside,
                jnp.where(lane == first + r, 1.0, 0.0),
                jnp.broadcast_to(blocks[b][r : r + 1, :], full),
            )
            for r in range(SUB)
        ]
        unit = [[None] * SUB for _ in range(SUB)]
        inverse = [None] * SUB
        for c in range(SUB):
            inverse[c] = 1.0 / upper[c][c]
            for r in range(c + 1, SUB):
                unit[c][r] = upper[c][r] * inverse[c]
                for j in range(r, SUB):
                    upper[r][j] = upper[r][j] - unit[c][r] * upper[c][j]
                rows[r] = rows[r] - unit[c][r] * rows[c]
        store(b, rows, upper, lane, sub)
        solved = [rows[r] * inverse[r] for r in range(SUB)]
        for c in range(SUB - 1, 0, -1):
            for r in range(c):
                solved[r] = solved[r] - unit[r][c] * solved[c]
        for i in range(b + 1, count):
            terms = [columns[i - b][c] * solved[c] for c in range(SUB)]
            while len(terms) > 1:
                terms = [terms[t] + terms[t + 1] for t in range(0, len(terms), 2)]
            blocks[i] = jnp.where(inside, 0.0, blocks[i]) - terms[0]


def basis_kernel(
    points,
    spans,
    gram_ref,
    filtered_hbm,
    basis_hbm,
    factor_hbm,
    filtered_ref,
    basis_ref,
    factor_ref,
    split,
    turned,
    load_sem,
    store_sem,
):
    size = gram_ref.shape[0]
    load = pltpu.make_async_copy(filtered_hbm, filtered_ref, load_sem)
    load.start()
    root = math.sqrt(points)

    def store(b, rows, upper, lane, sub):
        first = b * SUB
        block = rows[0]
        pivot = upper[0][0]
        for r in range(1, SUB):
            block = jnp.where(sub == r, rows[r], block)
            pivot = jnp.where(sub == r, upper[r][r], pivot)
        corner = block
        for r in range(SUB):
            for c in range(r, SUB):
                corner = jnp.where((sub == r) & (lane == first + c), upper[r][c], corner)
        diagonal = jnp.sqrt(pivot)
        here = slice(first, first + SUB)
        inverse = jnp.where(lane <= sub + first, block, 0.0) * (root / diagonal)
        top = inverse.astype(jnp.bfloat16).astype(jnp.float32)
        split[here, :] = top
        split[size + first : size + first + SUB, :] = inverse - top
        turned[here, :] = jnp.where(lane >= sub + first, corner, 0.0) / (diagonal * root)

    factor(gram_ref, store)
    load.wait()
    both_parts = split[...].astype(jnp.bfloat16)
    stores = []
    for index, (start, width) in enumerate(spans):
        rows = pl.ds(start, min(width, basis_ref.shape[0] - start))
        both = lax.dot_general(
            filtered_ref[rows, :],
            both_parts,
            (((1,), (1,)), ((), ())),
            preferred_element_type=jnp.float32,
        )
        basis_ref[rows, :] = both[:, :size] + both[:, size:]
        copy = pltpu.make_async_copy(
            basis_ref.at[rows], basis_hbm.at[rows], store_sem.at[index]
        )
        copy.start()
        stores.append(copy)
        if index == 0:
            factor_ref[...] = turned[...].T
            copy = pltpu.make_async_copy(factor_ref, factor_hbm, store_sem.at[len(spans)])
            copy.start()
            stores.append(copy)
    for copy in stores:
        copy.wait()


def paired_body(thermal_anomaly, smoothing_coefs):
    hours, sites = thermal_anomaly.shape
    total = 2 * hours
    half = sites // 2
    tiles = pl.cdiv(half, LANES)
    edge = max(1, tiles // (2 * CHUNKS))
    step = max(1, pl.cdiv(tiles - 2 * edge, CHUNKS - 2))
    cuts = [0, *range(edge, max(edge, tiles - edge), step), max(edge, tiles - edge), tiles]
    spans = [(a * LANES, (b - a) * LANES) for a, b in zip(cuts, cuts[1:]) if b > a]
    padded = tiles * LANES
    group = PLANE * 2
    lines = lax.axis_size("space") // PLANE
    share = total // group
    dma = pltpu.SemaphoreType.DMA
    vmem = pl.BlockSpec(memory_space=pltpu.VMEM)
    anywhere = pl.BlockSpec(memory_space=pl.ANY)
    filtered, gram = pl.pallas_call(
        functools.partial(gather_kernel, spans),
        out_shape=(
            jax.ShapeDtypeStruct((padded, total), jnp.bfloat16),
            jax.ShapeDtypeStruct((total, total), jnp.float32),
        ),
        in_specs=[pl.BlockSpec(memory_space=pltpu.HBM)] * 2,
        out_specs=(anywhere, vmem),
        scratch_shapes=[
            pltpu.VMEM((hours, sites), jnp.bfloat16),
            pltpu.VMEM((1, total), jnp.float32),
            pltpu.VMEM((padded, total), jnp.bfloat16),
            dma((SLABS + 1,)),
            dma((len(spans),)),
            pltpu.VMEM((hours, padded), jnp.bfloat16),
            pltpu.VMEM((total, padded), jnp.bfloat16),
            pltpu.VMEM((total, total), jnp.float32),
            pltpu.VMEM((group - 1, share, total), jnp.float32),
            pltpu.VMEM((share, total), jnp.float32),
            pltpu.VMEM((lines, share, total), jnp.float32),
            pltpu.VMEM((total, total), jnp.float32),
            dma((len(spans),)),
            dma((len(spans),)),
            dma((group - 1,)),
            dma((group - 1,)),
            dma((lines - 1,)),
            dma((lines - 1,)),
            dma((group - 1,)),
            dma((group - 1,)),
        ],
        compiler_params=pltpu.CompilerParams(
            collective_id=0, has_side_effects=True, vmem_limit_bytes=GRANT
        ),
        name="gather_gram",
    )(thermal_anomaly, smoothing_coefs[: total].reshape(1, total))

    points = sites * lax.axis_size("space")
    basis, lower = pl.pallas_call(
        functools.partial(basis_kernel, points, spans),
        out_shape=(
            jax.ShapeDtypeStruct((half, total), jnp.float32),
            jax.ShapeDtypeStruct((total, total), jnp.float32),
        ),
        in_specs=[vmem, anywhere],
        out_specs=(anywhere, anywhere),
        scratch_shapes=[
            pltpu.VMEM((padded, total), jnp.bfloat16),
            pltpu.VMEM((half, total), jnp.float32),
            pltpu.VMEM((total, total), jnp.float32),
            pltpu.VMEM((2 * total, total), jnp.float32),
            pltpu.VMEM((total, total), jnp.float32),
            dma,
            dma((len(spans) + 1,)),
        ],
        compiler_params=pltpu.CompilerParams(vmem_limit_bytes=GRANT),
        name="factor_basis",
    )(gram, filtered)
    return basis.T, lower


def body(thermal_anomaly, smoothing_coefs):
    hours, sites = thermal_anomaly.shape
    paired = (
        lax.axis_size("tm") == 2
        and 2 * hours == LANES
        and smoothing_coefs.shape[0] >= LANES
        and sites % 2 == 0
        and lax.axis_size("space") % PLANE == 0
        and lax.axis_size("space") > PLANE
    )
    return (paired_body if paired else general_body)(thermal_anomaly, smoothing_coefs)


def solution(mesh):
    placed = (P("tm", "space"), P())
    return jax.shard_map(
        body, mesh=mesh, in_specs=placed, out_specs=(P(None, ("space", "tm")), P()), check_vma=False
    )
```
